32 devices in a mesh: gx: 4 (over z), gy: 8 (over y, x, core).
Axes of the slice: x: 2, y: 2, z: 4, core: 2. Of those that a mesh axis runs over, the one named last changes fastest.
Arguments:
- vorticity: float32 [8192, 8192], P('gx', 'gy'), may hold values from -6 to 6
- tile_list: int32 [32, 16], P(('gx', 'gy')), may hold values from 0 to 4095, as said below
- float_slot: int32 [65536], P(('gx', 'gy')), may hold values from 0 to 15, as said below
- float_cell: int32 [2, 65536], P(None, ('gx', 'gy')), may hold values from 1 to 125
- float_frac: float32 [2, 65536], P(None, ('gx', 'gy')), may hold values from 0 to 1
Outputs:
- float_velocity: float32 [2, 65536], P(None, ('gx', 'gy'))
The draws below stay inside these ranges and needn't reach their ends.
Inputs may be any that keep to these rules, and one draw needn't show every extreme that they name: `tile_list`: row b lists the 16 tiles used by float block b; tile t covers the 128 x 128 cells from row (t // 64) * 128 and column (t % 64) * 128. The 16 tiles of a row lie in the blocks of vorticity held by 16 different devices, and one device's block is named by every row. `float_slot`: at most 256 floats of one block name the same position; in every block the position whose tile lies in the device block named by every row of tile_list is named by exactly 256 floats.
All inputs are finite; a program needn't handle non-finite values.
Results may differ from the reference program's by a relative error of at most 0.0031.
Values may be sent and summed in bfloat16 or wider, within the bound.
A program may use at most 128 MiB of HBM per device.

```python
import math
import jax
import jax.numpy as jnp
from jax import lax

N = 8192
TILE = 128
F_DEV = 2048
DRIFTER_GROUPS = 32
K = 16
FCAP = 256
FLOATS = 65536
TR = 16
TC = 8
TILES_DEV = 128
NTC = 64


def float_plan(key):
    base = jax.random.fold_in(key, 7)
    key_hot, key_score, random_lean, key_order = jax.random.split(base, 4)
    busiest_block = jax.random.randint(key_hot, (), 0, DRIFTER_GROUPS)
    owning_positions = jnp.arange(DRIFTER_GROUPS, dtype=jnp.int32)
    group_score = jax.random.randint(key_score, (DRIFTER_GROUPS, DRIFTER_GROUPS), 0, 65536)
    affinity_reward = jax.random.randint(random_lean, (DRIFTER_GROUPS,), 0, 4)
    added_reward = jnp.where(owning_positions == busiest_block, 1048576, 0)
    overall_total = (group_score + affinity_reward[None, :] * 16384 + added_reward[None, :]) * DRIFTER_GROUPS + owning_positions[None, :]
    chosen = lax.top_k(overall_total, K)[1].astype(jnp.int32)
    order_score = jax.random.randint(key_order, (DRIFTER_GROUPS, K), 0, 65536) * K + jnp.arange(K, dtype=jnp.int32)[None, :]
    order = lax.top_k(order_score, K)[1]
    owners = jnp.take_along_axis(chosen, order, axis=1)
    hot_slot = jnp.sum(jnp.where(owners == busiest_block, jnp.arange(K, dtype=jnp.int32)[None, :], 0), axis=1)
    return (owners, hot_slot)


def draw_tile_list(key, part):
    owners, hot_slot = float_plan(key)
    local_tile = jax.random.randint(jax.random.fold_in(key, 9), (DRIFTER_GROUPS, K), 0, TILES_DEV)
    group_cols = NTC // TC
    grid_row = owners // group_cols * TR + local_tile // TC
    grid_col = owners % group_cols * TC + local_tile % TC
    return (grid_row * NTC + grid_col).astype(jnp.int32)


def draw_float_slot(key, part):
    owners, hot_slot = float_plan(key)
    key_weight, key_order = jax.random.split(jax.random.fold_in(key, 13))
    weights = jax.random.randint(key_weight, (DRIFTER_GROUPS, K - 1), 2, 4)
    remainder = F_DEV - FCAP
    bounds = jnp.cumsum(weights * remainder, axis=1) // jnp.sum(weights, axis=1, keepdims=True)
    order_score = jax.random.randint(key_order, (DRIFTER_GROUPS, F_DEV), 0, 65536) * F_DEV + jnp.arange(F_DEV, dtype=jnp.int32)[None, :]
    order = lax.top_k(order_score, F_DEV)[1]
    turn = jnp.arange(F_DEV, dtype=jnp.int32)
    other = jnp.sum((bounds[:, None, :] <= (turn - FCAP)[None, :, None]).astype(jnp.int32), axis=2)
    other = other + (other >= hot_slot[:, None]).astype(jnp.int32)
    by_turn = jnp.where(turn[None, :] < FCAP, hot_slot[:, None], other)
    block_ids = jnp.broadcast_to(jnp.arange(DRIFTER_GROUPS, dtype=jnp.int32)[:, None], (DRIFTER_GROUPS, F_DEV))
    slots = jnp.zeros((DRIFTER_GROUPS, F_DEV), jnp.int32).at[block_ids, order].set(by_turn)
    return slots.reshape(DRIFTER_GROUPS * F_DEV).astype(jnp.int32)


def draw_vorticity(key, part):
    noise_key = jax.random.fold_in(key, 3)
    return jnp.clip(jax.random.normal(noise_key, (N, N), jnp.float32), -6.0, 6.0)


def with_ends(array, own_key, low, largest):
    shape = array.shape
    place = [jax.random.randint(jax.random.fold_in(own_key, axis), (), 0, shape[axis]) for axis in range(len(shape))]
    array = array.at[tuple(place)].set(low)
    longest = shape.index(max(shape))
    place[longest] = (place[longest] + 1) % shape[longest]
    return array.at[tuple(place)].set(largest)


def levels(stream_key, extent, pieces, low, largest):
    gain, own = 1.0, jax.random.fold_in(stream_key, 6)
    for dim, parts in pieces:
        steps = jnp.exp(jax.random.uniform(jax.random.fold_in(own, dim), (parts,), jnp.float32, low / len(pieces), largest / len(pieces)))
        gain = gain * jnp.repeat(steps, extent[dim] // parts).reshape([-1 if axis == dim else 1 for axis in range(len(extent))])
    return gain


def setup_inputs(seed: int = 0) -> dict:
    splits = jax.random.split(jax.random.key(seed), 6)
    return {
        "vorticity": draw_vorticity(jax.random.fold_in(splits[5], 71), 0),
        "tile_list": draw_tile_list(jax.random.fold_in(splits[5], 71), 0),
        "float_slot": draw_float_slot(jax.random.fold_in(splits[5], 71), 0),
        "float_cell": with_ends(jax.random.randint(splits[3], (2, FLOATS), 1, TILE - 2), jax.random.fold_in(splits[3], 1), 1, (TILE - 2) - 1).astype(jnp.int32),
        "float_frac": jnp.clip(1.0 * jax.random.uniform(splits[4], (2, FLOATS), jnp.float32) ** levels(splits[4], (2, FLOATS), ((1, 32),), -0.2, 0.2), 0.0, 1.0),
    }


def wavenumbers(index, length):
    signed = jnp.where(index < length // 2, index, index - length).astype(jnp.float32)
    wave = (2.0 * math.pi / length) * signed
    slope = jnp.where(index == length // 2, 0.0, wave)
    return wave, slope, (2.0 + jnp.cos(wave)) / 3.0


def spline_weights(position):
    complement = 1.0 - position
    cubed = position * position * position
    return (complement * complement * complement / 6.0,
            (3.0 * cubed - 6.0 * position * position + 4.0) / 6.0,
            (-3.0 * cubed + 3.0 * position * position + 3.0 * position + 1.0) / 6.0,
            cubed / 6.0)


def reference(vorticity, tile_list, float_slot, float_cell, float_frac):
    length = vorticity.shape[0]
    spectrum = jnp.fft.rfft2(vorticity)
    row_wave, row_slope, row_prefilter = wavenumbers(jnp.arange(length, dtype=jnp.int32), length)
    col_wave, col_slope, col_prefilter = wavenumbers(jnp.arange(length // 2 + 1, dtype=jnp.int32), length)
    kappa = math.pi / length
    factor = 1.0 / ((row_wave[:, None] * row_wave[:, None] + col_wave[None, :] * col_wave[None, :] + kappa * kappa)
                    * (row_prefilter[:, None] * col_prefilter[None, :]))
    spec_u = 1j * (row_slope[:, None] * factor) * spectrum
    spec_v = -1j * (col_slope[None, :] * factor) * spectrum
    coeff_u = jnp.fft.irfft2(spec_u, s=(length, length)).astype(jnp.float32)
    coeff_v = jnp.fft.irfft2(spec_v, s=(length, length)).astype(jnp.float32)
    coeffs = lax.optimization_barrier(jnp.stack([coeff_u, coeff_v]).astype(jnp.bfloat16))
    per_row = length // TILE
    float_count = float_slot.shape[0]
    block_len = float_count // tile_list.shape[0]
    owner_block = jnp.arange(float_count, dtype=jnp.int32) // block_len
    tile_number = tile_list[owner_block, float_slot]
    row_start = (tile_number // per_row) * TILE + float_cell[0] - 1
    col_start = (tile_number % per_row) * TILE + float_cell[1] - 1
    offsets = jnp.arange(4, dtype=jnp.int32)
    row_cells = row_start[:, None] + offsets[None, :]
    col_cells = col_start[:, None] + offsets[None, :]
    window = coeffs[:, row_cells[:, :, None], col_cells[:, None, :]]
    down = lax.optimization_barrier(jnp.stack(spline_weights(float_frac[0]), axis=1).astype(jnp.bfloat16))
    across = jnp.stack(spline_weights(float_frac[1]), axis=1)
    inner = jnp.einsum("fi,cfij->cfj", down.astype(jnp.float32), window.astype(jnp.float32))
    return jnp.einsum("fj,cfj->cf", across, inner)
```

```python
import math

import jax
import jax.numpy as jnp
import numpy as np
from jax import lax
from jax.sharding import PartitionSpec as P

TILE = 128
HIGH = lax.Precision.HIGH
F32 = jnp.float32
BF16 = jnp.bfloat16
F16 = jnp.float16


def root(height, width, modulus, sign):
    product = np.arange(height)[:, None] * np.arange(width)[None, :] % modulus
    angle = sign * 2.0 * math.pi / modulus * product
    return np.cos(angle), np.sin(angle)


def mixing(height, width, modulus, sign):
    real, imag = root(height, width, modulus, sign)
    return np.stack([np.stack([real, imag], 1), np.stack([-imag, real], 1)]).astype(np.float32)


def twiddle_table(height, width, modulus, sign):
    product = (
        jnp.arange(height, dtype=jnp.int32)[:, None]
        * jnp.arange(width, dtype=jnp.int32)[None, :]
        % modulus
    )
    angle = sign * 2.0 * math.pi / modulus * product.astype(F32)
    return jnp.cos(angle), jnp.sin(angle)


def dot(formula, left, right):
    return jnp.einsum(formula, left, right, precision=HIGH, preferred_element_type=F32)


def turned(values, table, axis_shape):
    real, imag = (part.reshape(axis_shape) for part in table)
    return jnp.stack(
        [values[0] * real - values[1] * imag, values[0] * imag + values[1] * real]
    )


def mirrored(values):
    return jnp.roll(jnp.flip(values, -1), 1, -1)


def wavenumbers(index, length):
    signed = jnp.where(index < length // 2, index, index - length).astype(F32)
    wave = 2.0 * math.pi / length * signed
    slope = jnp.where(index == length // 2, 0.0, wave)
    return (wave, slope, (2.0 + jnp.cos(wave)) / 3.0)


def multipliers(row_index, col_index, length):
    row_wave, row_slope, row_prefilter = wavenumbers(row_index, length)
    col_wave, col_slope, col_prefilter = wavenumbers(col_index, length)
    kappa = math.pi / length
    factor = 1.0 / (
        (row_wave * row_wave + col_wave * col_wave + kappa * kappa)
        * (row_prefilter * col_prefilter)
    )
    return row_slope * factor, col_slope * factor


def spline_weights(position):
    complement = 1.0 - position
    cubed = position * position * position
    return (
        complement * complement * complement / 6.0,
        (3.0 * cubed - 6.0 * position * position + 4.0) / 6.0,
        (-3.0 * cubed + 3.0 * position * position + 3.0 * position + 1.0) / 6.0,
        cubed / 6.0,
    )


def dense_weights(start, position, width):
    cells = jnp.arange(width, dtype=jnp.int32)
    overall_total = jnp.zeros(start.shape + (width,), F32)
    for offset, weight in enumerate(spline_weights(position)):
        overall_total = overall_total + jnp.where(
            cells == (start + offset)[..., None], weight[..., None], 0.0
        )
    return overall_total


def slot_velocity(chosen_tiles, cells, fractions):
    width = chosen_tiles.shape[-1]
    down = dense_weights(cells[:, 0] - 1, fractions[:, 0], width).astype(BF16)
    across = dense_weights(cells[:, 1] - 1, fractions[:, 1], width)
    inner = jnp.einsum("scr,sdtr->sdct", down, chosen_tiles, preferred_element_type=F32)
    return jnp.sum(inner * across[:, None], axis=-1)


def shards(vorticity, tile_list, float_slot, float_cell, float_frac):
    both = ("gx", "gy")
    group_cols = lax.axis_size("gy")
    devices = lax.axis_size(both)
    my_index = lax.axis_index(both)
    block_rows, block_cols = vorticity.shape
    length = block_cols * group_cols
    rows = length // devices
    cols = length // 2 // devices
    low = TILE
    high = length // low
    half_low = low // 2
    alternating = jnp.asarray(1.0 - 2.0 * (np.arange(low) % 2), F32)

    slab = vorticity.astype(F16).reshape(group_cols, rows, block_cols)
    slab = lax.all_to_all(slab, "gy", split_axis=0, concat_axis=0)
    slab = slab.reshape(group_cols, rows, block_cols // low, low)
    real, imag = root(high, high, high, -1.0)
    table = np.stack([real, imag], 1).reshape(group_cols, block_cols // low, 2, high)
    first = dot("hgck,hrgb->ckrb", table.astype(np.float32), slab.astype(F32))
    twist = twiddle_table(high, low, length, -1.0)
    nyquist = jnp.sum(first[0, 0] * alternating[None, :], axis=-1)
    first = turned(first, twist, (high, 1, low))
    spec = dot("cbdm,ckrb->dmkr", mixing(low, half_low, low, -1.0), first)
    here = jnp.logical_and(
        jnp.arange(half_low)[:, None] == 0, jnp.arange(high)[None, :] == 0
    )[:, :, None]
    spec = jnp.stack([spec[0], jnp.where(here, nyquist[None, None, :], spec[1])])
    sent = (spec * 0.125).reshape(2, devices, cols, rows).astype(F16)
    sent = lax.all_to_all(sent, both, split_axis=1, concat_axis=0)

    if rows % low == 0:
        got = sent.reshape(devices, 2, cols, rows // low, low)
        table = mixing(high, high, high, -1.0).reshape(2, devices, rows // low, 2, high)
        second = dot("csgdk,scngb->dknb", table, got.astype(F32) * 8.0)
    else:
        got = sent.reshape(high, low // rows, 2, cols, rows).transpose(0, 2, 3, 1, 4)
        got = got.reshape(high, 2, cols, low)
        second = dot("cadk,acnb->dknb", mixing(high, high, high, -1.0), got.astype(F32) * 8.0)
    second = turned(second, twist, (high, 1, low))
    full = dot("cbdm,cknb->dknm", mixing(low, low, low, -1.0), second)

    row_index = (
        jnp.arange(high, dtype=jnp.int32)[:, None, None]
        + high * jnp.arange(low, dtype=jnp.int32)[None, None, :]
    )
    col_index = (my_index * cols + jnp.arange(cols, dtype=jnp.int32))[None, :, None]
    row_gain, col_gain = multipliers(row_index, col_index, length)
    row_gain = row_gain * 2.0
    col_gain = col_gain * 2.0
    u_real, u_imag = -row_gain * full[1], row_gain * full[0]
    v_real, v_imag = col_gain * full[1], -col_gain * full[0]

    edge_real = full[0, :, 0].T.reshape(length)
    edge_imag = full[1, :, 0].T.reshape(length)
    flip_real = mirrored(edge_real)
    flip_imag = mirrored(edge_imag)
    ends_real = jnp.stack([(edge_real + flip_real) * 0.5, (edge_imag + flip_imag) * 0.5])
    ends_imag = jnp.stack([(edge_imag - flip_imag) * 0.5, -(edge_real - flip_real) * 0.5])
    end_row, end_col = multipliers(
        jnp.arange(length, dtype=jnp.int32)[None, :],
        jnp.array([0, length // 2], dtype=jnp.int32)[:, None],
        length,
    )
    eu_real, eu_imag = -end_row * ends_imag, end_row * ends_real
    ev_real, ev_imag = end_col * ends_imag, -end_col * ends_real
    on_edge = jnp.logical_and(my_index == 0, jnp.arange(cols) == 0)[None, :, None]

    def place(edge, values):
        return jnp.where(on_edge, edge.reshape(low, high).T[:, None, :], values)

    fields = jnp.stack(
        [
            jnp.stack([place(eu_real[0] - eu_imag[1], u_real), place(ev_real[0] - ev_imag[1], v_real)]),
            jnp.stack([place(eu_imag[0] + eu_real[1], u_imag), place(ev_imag[0] + ev_real[1], v_imag)]),
        ]
    )

    third = dot("cmdb,cfknm->dfknb", mixing(low, low, low, 1.0), fields)
    untwist = twiddle_table(high, low, length, 1.0)
    third = turned(third, untwist, (1, high, 1, low))
    back = dot("ckda,cfknb->adfnb", mixing(high, high, high, 1.0), third)
    back = back.astype(BF16)
    if rows % low == 0:
        back = back.reshape(devices, rows // low, 2, 2, cols, low)
    else:
        back = back.reshape(high, 2, 2, cols, low // rows, rows).transpose(0, 4, 1, 2, 3, 5)
        back = back.reshape(devices, 1, 2, 2, cols, rows)
    back = lax.all_to_all(back, both, split_axis=0, concat_axis=0)

    groups, lanes = back.shape[1], back.shape[-1]
    if cols % high == 0:
        back = back.reshape(devices * groups, 2, 2, cols // high, high, lanes)
        back = back.reshape(devices, groups, 2, 2, cols // high, high, lanes)
        table = mixing(half_low, low, low, 1.0).reshape(2, devices, cols // high, 2, low)
        fourth = dot("csmdb,sgcfmky->dgfkby", table, back.astype(F32))
        nyquist = back[0, :, 1, :, 0, 0]
    else:
        back = back.reshape(half_low, high // cols, groups, 2, 2, cols, lanes)
        back = back.transpose(0, 2, 3, 4, 1, 5, 6).reshape(half_low, groups, 2, 2, high, lanes)
        fourth = dot("cmdb,mgcfky->dgfkby", mixing(half_low, low, low, 1.0), back.astype(F32))
        nyquist = back[0, :, 1, :, 0]
    lift = nyquist.astype(F32)[:, :, None, None, :] * alternating[None, None, None, :, None]
    first_k = (jnp.arange(high) == 0)[None, None, :, None, None]
    fourth = jnp.stack([fourth[0] + jnp.where(first_k, lift, 0.0), fourth[1]])
    fourth = turned(fourth, untwist, (1, 1, high, low, 1))
    real, imag = root(high, high, high, 1.0)
    table = np.stack([real, -imag]).astype(np.float32) / (length * length)
    coeffs = dot("cka,cgfkby->agfby", table, fourth).astype(BF16)
    tile_rows = block_rows // TILE
    tile_cols = block_cols // TILE
    coeffs = coeffs.reshape(group_cols, tile_cols * groups, 2, TILE, lanes)
    tiles = lax.all_to_all(coeffs, "gy", split_axis=0, concat_axis=0)
    if lanes == TILE:
        tiles = tiles.reshape(group_cols, tile_cols, groups, 2, TILE, TILE)
        tile_groups = groups
    else:
        parts = TILE // lanes
        tiles = tiles.reshape(group_cols // parts, parts, tile_cols, 2, TILE, lanes)
        tiles = tiles.transpose(0, 2, 3, 4, 1, 5)
        tile_groups = 1
    tiles = tiles.reshape(tile_rows * tile_cols, 2, TILE, TILE)

    wanted = tile_list[0]
    tile_count = wanted.shape[0]
    per_row = length // TILE
    grid_row = wanted // per_row
    grid_col = wanted % per_row
    owner_index = grid_row // tile_rows * group_cols + grid_col // tile_cols
    local_row = grid_row % tile_rows
    local_index = (
        local_row // tile_groups * tile_cols + grid_col % tile_cols
    ) * tile_groups + local_row % tile_groups
    float_total = float_slot.shape[0]
    capacity = 2 * float_total // tile_count
    member = (float_slot[:, None] == jnp.arange(tile_count, dtype=jnp.int32)[None, :]).astype(
        jnp.int32
    )
    slot_rank = jnp.sum((jnp.cumsum(member, axis=0) - member) * member, axis=1)
    placing = float_slot * capacity + slot_rank
    grouped_cell = jnp.zeros((2, tile_count * capacity), jnp.int32).at[:, placing].set(float_cell)
    grouped_cell = grouped_cell.reshape(2, tile_count, capacity).transpose(1, 0, 2)
    grouped_frac = jnp.zeros((2, tile_count * capacity), F32).at[:, placing].set(float_frac)
    grouped_frac = grouped_frac.reshape(2, tile_count, capacity).transpose(1, 0, 2)
    owns = (owner_index[:, None] == jnp.arange(devices, dtype=jnp.int32)[None, :]).astype(jnp.int32)
    request = jnp.sum(owns * (local_index[:, None] + 1), axis=0) - 1
    request = lax.all_to_all(request, both, split_axis=0, concat_axis=0, tiled=True)
    outgoing = jnp.take(tiles, jnp.maximum(request, 0), axis=0)
    incoming = lax.all_to_all(outgoing, both, split_axis=0, concat_axis=0, tiled=True)
    grouped = slot_velocity(jnp.take(incoming, owner_index, axis=0), grouped_cell, grouped_frac)
    flattened = grouped.transpose(1, 0, 2).reshape(2, tile_count * capacity)
    return jnp.take(flattened, placing, axis=1)


def solution(mesh):
    in_specs = (
        P("gx", "gy"),
        P(("gx", "gy"), None),
        P(("gx", "gy")),
        P(None, ("gx", "gy")),
        P(None, ("gx", "gy")),
    )
    out_specs = P(None, ("gx", "gy"))
    return jax.shard_map(shards, mesh=mesh, in_specs=in_specs, out_specs=out_specs, check_vma=False)
```

```python
import math

import jax
import jax.numpy as jnp
import numpy as np
from jax import lax
from jax.sharding import PartitionSpec as P

TILE = 128
HIGH = lax.Precision.HIGH
F32 = jnp.float32
BF16 = jnp.bfloat16
F16 = jnp.float16


def root(height, width, modulus, sign):
    product = np.arange(height)[:, None] * np.arange(width)[None, :] % modulus
    angle = sign * 2.0 * math.pi / modulus * product
    return np.cos(angle), np.sin(angle)


def mixing(height, width, modulus, sign):
    real, imag = root(height, width, modulus, sign)
    return np.stack([np.stack([real, imag], 1), np.stack([-imag, real], 1)]).astype(np.float32)


def twiddle_table(height, width, modulus, sign):
    product = (
        jnp.arange(height, dtype=jnp.int32)[:, None]
        * jnp.arange(width, dtype=jnp.int32)[None, :]
        % modulus
    )
    angle = sign * 2.0 * math.pi / modulus * product.astype(F32)
    return jnp.cos(angle), jnp.sin(angle)


def dot(formula, left, right):
    return jnp.einsum(formula, left, right, precision=HIGH, preferred_element_type=F32)


def turned(values, table, axis_shape):
    real, imag = (part.reshape(axis_shape) for part in table)
    return jnp.stack(
        [values[0] * real - values[1] * imag, values[0] * imag + values[1] * real]
    )


def mirrored(values):
    return jnp.roll(jnp.flip(values, -1), 1, -1)


def wavenumbers(index, length):
    signed = jnp.where(index < length // 2, index, index - length).astype(F32)
    wave = 2.0 * math.pi / length * signed
    slope = jnp.where(index == length // 2, 0.0, wave)
    return (wave, slope, (2.0 + jnp.cos(wave)) / 3.0)


def multipliers(row_index, col_index, length):
    row_wave, row_slope, row_prefilter = wavenumbers(row_index, length)
    col_wave, col_slope, col_prefilter = wavenumbers(col_index, length)
    kappa = math.pi / length
    factor = 1.0 / (
        (row_wave * row_wave + col_wave * col_wave + kappa * kappa)
        * (row_prefilter * col_prefilter)
    )
    return row_slope * factor, col_slope * factor


def spline_weights(position):
    complement = 1.0 - position
    cubed = position * position * position
    return (
        complement * complement * complement / 6.0,
        (3.0 * cubed - 6.0 * position * position + 4.0) / 6.0,
        (-3.0 * cubed + 3.0 * position * position + 3.0 * position + 1.0) / 6.0,
        cubed / 6.0,
    )


def dense_weights(start, position, width):
    cells = jnp.arange(width, dtype=jnp.int32)
    overall_total = jnp.zeros(start.shape + (width,), F32)
    for offset, weight in enumerate(spline_weights(position)):
        overall_total = overall_total + jnp.where(
            cells == (start + offset)[..., None], weight[..., None], 0.0
        )
    return overall_total


def slot_velocity(chosen_tiles, cells, fractions):
    width = chosen_tiles.shape[-1]
    down = dense_weights(cells[:, 0] - 1, fractions[:, 0], width).astype(BF16)
    across = dense_weights(cells[:, 1] - 1, fractions[:, 1], width)
    inner = jnp.einsum("scr,sdtr->sdct", down, chosen_tiles, preferred_element_type=F32)
    return jnp.sum(inner * across[:, None], axis=-1)


def shards(vorticity, tile_list, float_slot, float_cell, float_frac):
    both = ("gx", "gy")
    group_cols = lax.axis_size("gy")
    devices = lax.axis_size(both)
    my_index = lax.axis_index(both)
    block_rows, block_cols = vorticity.shape
    length = block_cols * group_cols
    rows = length // devices
    cols = length // 2 // devices
    low = TILE
    high = length // low
    half_low = low // 2
    alternating = jnp.asarray(1.0 - 2.0 * (np.arange(low) % 2), F32)

    chunks = rows // low if rows % low == 0 else 1
    piece = rows // chunks
    real, imag = root(high, high, high, -1.0)
    row_table = np.stack([real, imag], 1).reshape(group_cols, block_cols // low, 2, high)
    row_table = row_table.astype(np.float32)
    twist = twiddle_table(high, low, length, -1.0)
    here = jnp.logical_and(
        jnp.arange(half_low)[:, None] == 0, jnp.arange(high)[None, :] == 0
    )[:, :, None]
    blocks = vorticity.reshape(group_cols, chunks, piece, block_cols)
    slabs = [
        lax.all_to_all(blocks[:, chunk].astype(F16), "gy", split_axis=0, concat_axis=0)
        for chunk in range(chunks)
    ]
    if chunks > 1:
        col_table = mixing(high, high, high, -1.0).reshape(2, devices, chunks, 2, high)
    second = None
    for chunk in range(chunks):
        slab = slabs[chunk]
        slab = slab.reshape(group_cols, piece, block_cols // low, low)
        first = dot("hgck,hrgb->ckrb", row_table, slab.astype(F32))
        nyquist = jnp.sum(first[0, 0] * alternating[None, :], axis=-1)
        first = turned(first, twist, (high, 1, low))
        spec = dot("cbdm,ckrb->dmkr", mixing(low, half_low, low, -1.0), first)
        spec = jnp.stack([spec[0], jnp.where(here, nyquist[None, None, :], spec[1])])
        sent = (spec * 0.125).reshape(2, devices, cols, piece).astype(F16)
        if chunk + 1 < chunks:
            sent, slabs[chunk + 1] = lax.optimization_barrier((sent, slabs[chunk + 1]))
        sent = lax.all_to_all(sent, both, split_axis=1, concat_axis=0)
        if rows % low == 0:
            got = sent.reshape(devices, 2, cols, low).astype(F32) * 8.0
            table = (
                mixing(high, high, high, -1.0).reshape(2, devices, 2, high)
                if chunks == 1
                else col_table[:, :, chunk]
            )
            part = dot("csdk,scnb->dknb", table, got)
        else:
            got = sent.reshape(high, low // rows, 2, cols, rows).transpose(0, 2, 3, 1, 4)
            got = got.reshape(high, 2, cols, low).astype(F32) * 8.0
            part = dot("cadk,acnb->dknb", mixing(high, high, high, -1.0), got)
        second = part if second is None else second + part
    second = turned(second, twist, (high, 1, low))
    full = dot("cbdm,cknb->dknm", mixing(low, low, low, -1.0), second)

    row_index = (
        jnp.arange(high, dtype=jnp.int32)[:, None, None]
        + high * jnp.arange(low, dtype=jnp.int32)[None, None, :]
    )
    col_index = (my_index * cols + jnp.arange(cols, dtype=jnp.int32))[None, :, None]
    row_gain, col_gain = multipliers(row_index, col_index, length)
    row_gain = row_gain * 2.0
    col_gain = col_gain * 2.0
    u_real, u_imag = -row_gain * full[1], row_gain * full[0]
    v_real, v_imag = col_gain * full[1], -col_gain * full[0]

    edge_real = full[0, :, 0].T.reshape(length)
    edge_imag = full[1, :, 0].T.reshape(length)
    flip_real = mirrored(edge_real)
    flip_imag = mirrored(edge_imag)
    ends_real = jnp.stack([(edge_real + flip_real) * 0.5, (edge_imag + flip_imag) * 0.5])
    ends_imag = jnp.stack([(edge_imag - flip_imag) * 0.5, -(edge_real - flip_real) * 0.5])
    end_row, end_col = multipliers(
        jnp.arange(length, dtype=jnp.int32)[None, :],
        jnp.array([0, length // 2], dtype=jnp.int32)[:, None],
        length,
    )
    eu_real, eu_imag = -end_row * ends_imag, end_row * ends_real
    ev_real, ev_imag = end_col * ends_imag, -end_col * ends_real
    on_edge = jnp.logical_and(my_index == 0, jnp.arange(cols) == 0)[None, :, None]

    def place(edge, values):
        return jnp.where(on_edge, edge.reshape(low, high).T[:, None, :], values)

    fields = (
        jnp.stack([place(eu_real[0] - eu_imag[1], u_real), place(eu_imag[0] + eu_real[1], u_imag)]),
        jnp.stack([place(ev_real[0] - ev_imag[1], v_real), place(ev_imag[0] + ev_real[1], v_imag)]),
    )
    untwist = twiddle_table(high, low, length, 1.0)
    real, imag = root(high, high, high, 1.0)
    end_table = np.stack([real, -imag]).astype(np.float32) / (length * length)
    first_k = (jnp.arange(high) == 0)[None, :, None, None]
    tile_rows = block_rows // TILE
    tile_cols = block_cols // TILE

    def columns_back(field):
        third = dot("cmdb,cknm->dknb", mixing(low, low, low, 1.0), field)
        third = turned(third, untwist, (high, 1, low))
        back = dot("ckda,cknb->adnb", mixing(high, high, high, 1.0), third).astype(BF16)
        if rows % low == 0:
            back = back.reshape(devices, rows // low, 2, cols, low)
        else:
            back = back.reshape(high, 2, cols, low // rows, rows).transpose(0, 3, 1, 2, 4)
            back = back.reshape(devices, 1, 2, cols, rows)
        return lax.all_to_all(back, both, split_axis=0, concat_axis=0)

    def rows_back(back, later):
        groups, lanes = back.shape[1], back.shape[-1]
        if cols % high == 0:
            back = back.reshape(devices, groups, 2, cols // high, high, lanes)
            table = mixing(half_low, low, low, 1.0).reshape(2, devices, cols // high, 2, low)
            fourth = dot("csmdb,sgcmky->dgkby", table, back.astype(F32))
            nyquist = back[0, :, 1, 0, 0]
        else:
            back = back.reshape(half_low, high // cols, groups, 2, cols, lanes)
            back = back.transpose(0, 2, 3, 1, 4, 5).reshape(half_low, groups, 2, high, lanes)
            fourth = dot("cmdb,mgcky->dgkby", mixing(half_low, low, low, 1.0), back.astype(F32))
            nyquist = back[0, :, 1, 0]
        lift = nyquist.astype(F32)[:, None, None, :] * alternating[None, None, :, None]
        fourth = jnp.stack([fourth[0] + jnp.where(first_k, lift, 0.0), fourth[1]])
        fourth = turned(fourth, untwist, (1, high, low, 1))
        coeffs = dot("cka,cgkby->agby", end_table, fourth).astype(BF16)
        coeffs = coeffs.reshape(group_cols, tile_cols * groups, TILE, lanes)
        if later is not None:
            coeffs, later = lax.optimization_barrier((coeffs, later))
        tiles = lax.all_to_all(coeffs, "gy", split_axis=0, concat_axis=0)
        if lanes != TILE:
            parts = TILE // lanes
            tiles = tiles.reshape(group_cols // parts, parts, tile_cols, TILE, lanes)
            tiles = tiles.transpose(0, 2, 3, 1, 4)
        return tiles.reshape(tile_rows * tile_cols, TILE, TILE), later

    received = [columns_back(field) for field in fields]
    u_tiles, waiting = rows_back(received[0], received[1])
    v_tiles, _ = rows_back(waiting, None)
    tiles = [u_tiles, v_tiles]
    tile_groups = rows // TILE if rows % TILE == 0 else 1

    wanted = tile_list[0]
    tile_count = wanted.shape[0]
    per_row = length // TILE
    grid_row = wanted // per_row
    grid_col = wanted % per_row
    owner_index = grid_row // tile_rows * group_cols + grid_col // tile_cols
    local_row = grid_row % tile_rows
    local_index = (
        local_row // tile_groups * tile_cols + grid_col % tile_cols
    ) * tile_groups + local_row % tile_groups
    float_total = float_slot.shape[0]
    capacity = 2 * float_total // tile_count
    member = (float_slot[:, None] == jnp.arange(tile_count, dtype=jnp.int32)[None, :]).astype(
        jnp.int32
    )
    slot_rank = jnp.sum((jnp.cumsum(member, axis=0) - member) * member, axis=1)
    placing = float_slot * capacity + slot_rank
    grouped_cell = jnp.zeros((2, tile_count * capacity), jnp.int32).at[:, placing].set(float_cell)
    grouped_cell = grouped_cell.reshape(2, tile_count, capacity).transpose(1, 0, 2)
    grouped_frac = jnp.zeros((2, tile_count * capacity), F32).at[:, placing].set(float_frac)
    grouped_frac = grouped_frac.reshape(2, tile_count, capacity).transpose(1, 0, 2)
    owns = (owner_index[:, None] == jnp.arange(devices, dtype=jnp.int32)[None, :]).astype(jnp.int32)
    request = jnp.sum(owns * (local_index[:, None] + 1), axis=0) - 1
    request = lax.all_to_all(request, both, split_axis=0, concat_axis=0, tiled=True)
    asked = jnp.maximum(request, 0)
    outgoing = jnp.stack([jnp.take(part, asked, axis=0) for part in tiles], axis=1)
    incoming = lax.all_to_all(outgoing, both, split_axis=0, concat_axis=0, tiled=True)
    grouped = slot_velocity(jnp.take(incoming, owner_index, axis=0), grouped_cell, grouped_frac)
    flattened = grouped.transpose(1, 0, 2).reshape(2, tile_count * capacity)
    return jnp.take(flattened, placing, axis=1)


def solution(mesh):
    in_specs = (
        P("gx", "gy"),
        P(("gx", "gy"), None),
        P(("gx", "gy")),
        P(None, ("gx", "gy")),
        P(None, ("gx", "gy")),
    )
    out_specs = P(None, ("gx", "gy"))
    return jax.shard_map(shards, mesh=mesh, in_specs=in_specs, out_specs=out_specs, check_vma=False)
```

```python
import math

import jax
import jax.numpy as jnp
import numpy as np
from jax import lax
from jax.sharding import PartitionSpec as P

TILE = 128
HIGH = lax.Precision.HIGH
F32 = jnp.float32
BF16 = jnp.bfloat16
F16 = jnp.float16


def root(height, width, modulus, sign):
    product = np.arange(height)[:, None] * np.arange(width)[None, :] % modulus
    angle = sign * 2.0 * math.pi / modulus * product
    return np.cos(angle), np.sin(angle)


def mixing(height, width, modulus, sign):
    real, imag = root(height, width, modulus, sign)
    return np.stack([np.stack([real, imag], 1), np.stack([-imag, real], 1)]).astype(np.float32)


def twiddle_table(height, width, modulus, sign):
    product = (
        jnp.arange(height, dtype=jnp.int32)[:, None]
        * jnp.arange(width, dtype=jnp.int32)[None, :]
        % modulus
    )
    angle = sign * 2.0 * math.pi / modulus * product.astype(F32)
    return jnp.cos(angle), jnp.sin(angle)


def dot(formula, left, right):
    return jnp.einsum(formula, left, right, precision=HIGH, preferred_element_type=F32)


def turned(values, table, axis_shape):
    real, imag = (part.reshape(axis_shape) for part in table)
    return jnp.stack(
        [values[0] * real - values[1] * imag, values[0] * imag + values[1] * real]
    )


def mirrored(values):
    return jnp.roll(jnp.flip(values, -1), 1, -1)


def wavenumbers(index, length):
    signed = jnp.where(index < length // 2, index, index - length).astype(F32)
    wave = 2.0 * math.pi / length * signed
    slope = jnp.where(index == length // 2, 0.0, wave)
    return (wave, slope, (2.0 + jnp.cos(wave)) / 3.0)


def multipliers(row_index, col_index, length):
    row_wave, row_slope, row_prefilter = wavenumbers(row_index, length)
    col_wave, col_slope, col_prefilter = wavenumbers(col_index, length)
    kappa = math.pi / length
    factor = 1.0 / (
        (row_wave * row_wave + col_wave * col_wave + kappa * kappa)
        * (row_prefilter * col_prefilter)
    )
    return row_slope * factor, col_slope * factor


def spline_weights(position):
    complement = 1.0 - position
    cubed = position * position * position
    return (
        complement * complement * complement / 6.0,
        (3.0 * cubed - 6.0 * position * position + 4.0) / 6.0,
        (-3.0 * cubed + 3.0 * position * position + 3.0 * position + 1.0) / 6.0,
        cubed / 6.0,
    )


def dense_weights(start, position, width):
    cells = jnp.arange(width, dtype=jnp.int32)
    overall_total = jnp.zeros(start.shape + (width,), F32)
    for offset, weight in enumerate(spline_weights(position)):
        overall_total = overall_total + jnp.where(
            cells == (start + offset)[..., None], weight[..., None], 0.0
        )
    return overall_total


def slot_velocity(chosen_tiles, cells, fractions):
    width = chosen_tiles.shape[-1]
    down = dense_weights(cells[:, 0] - 1, fractions[:, 0], width).astype(BF16)
    across = dense_weights(cells[:, 1] - 1, fractions[:, 1], width)
    inner = jnp.einsum("scr,sdtr->sdct", down, chosen_tiles, preferred_element_type=F32)
    return jnp.sum(inner * across[:, None], axis=-1)


def shards(vorticity, tile_list, float_slot, float_cell, float_frac):
    both = ("gx", "gy")
    group_cols = lax.axis_size("gy")
    devices = lax.axis_size(both)
    my_index = lax.axis_index(both)
    block_rows, block_cols = vorticity.shape
    length = block_cols * group_cols
    rows = length // devices
    cols = length // 2 // devices
    low = TILE
    high = length // low
    half_low = low // 2
    alternating = jnp.asarray(1.0 - 2.0 * (np.arange(low) % 2), F32)

    chunks = rows // low if rows % low == 0 else 1
    piece = rows // chunks
    real, imag = root(high, high, high, -1.0)
    row_table = np.stack([real, imag], 1).reshape(group_cols, block_cols // low, 2, high)
    row_table = row_table.astype(np.float32)
    twist = twiddle_table(high, low, length, -1.0)
    here = jnp.logical_and(
        jnp.arange(half_low)[:, None] == 0, jnp.arange(high)[None, :] == 0
    )[:, :, None]
    blocks = vorticity.reshape(group_cols, chunks, piece, block_cols)
    slabs = [
        lax.all_to_all(blocks[:, chunk].astype(F16), "gy", split_axis=0, concat_axis=0)
        for chunk in range(chunks)
    ]
    if chunks > 1:
        col_table = mixing(high, high, high, -1.0).reshape(2, devices, chunks, 2, high)
    second = None
    for chunk in range(chunks):
        slab = slabs[chunk]
        slab = slab.reshape(group_cols, piece, block_cols // low, low)
        first = dot("hgck,hrgb->ckrb", row_table, slab.astype(F32))
        nyquist = jnp.sum(first[0, 0] * alternating[None, :], axis=-1)
        first = turned(first, twist, (high, 1, low))
        spec = dot("cbdm,ckrb->dmkr", mixing(low, half_low, low, -1.0), first)
        spec = jnp.stack([spec[0], jnp.where(here, nyquist[None, None, :], spec[1])])
        sent = (spec * 0.125).reshape(2, devices, cols, piece).astype(F16)
        if chunk + 1 < chunks:
            sent, slabs[chunk + 1] = lax.optimization_barrier((sent, slabs[chunk + 1]))
        sent = lax.all_to_all(sent, both, split_axis=1, concat_axis=0)
        if rows % low == 0:
            got = sent.reshape(devices, 2, cols, low).astype(F32) * 8.0
            table = (
                mixing(high, high, high, -1.0).reshape(2, devices, 2, high)
                if chunks == 1
                else col_table[:, :, chunk]
            )
            part = dot("csdk,scnb->dknb", table, got)
        else:
            got = sent.reshape(high, low // rows, 2, cols, rows).transpose(0, 2, 3, 1, 4)
            got = got.reshape(high, 2, cols, low).astype(F32) * 8.0
            part = dot("cadk,acnb->dknb", mixing(high, high, high, -1.0), got)
        second = part if second is None else second + part
    second = turned(second, twist, (high, 1, low))
    full = dot("cbdm,cknb->dknm", mixing(low, low, low, -1.0), second)

    tile_rows = block_rows // TILE
    tile_cols = block_cols // TILE
    tile_groups = rows // TILE if rows % TILE == 0 else 1
    wanted = tile_list[0]
    tile_count = wanted.shape[0]
    per_row = length // TILE
    grid_row = wanted // per_row
    grid_col = wanted % per_row
    owner_index = grid_row // tile_rows * group_cols + grid_col // tile_cols
    local_row = grid_row % tile_rows
    local_index = (
        local_row // tile_groups * tile_cols + grid_col % tile_cols
    ) * tile_groups + local_row % tile_groups
    owns = (owner_index[:, None] == jnp.arange(devices, dtype=jnp.int32)[None, :]).astype(jnp.int32)
    request = jnp.sum(owns * (local_index[:, None] + 1), axis=0) - 1
    request = lax.all_to_all(request, both, split_axis=0, concat_axis=0, tiled=True)
    full, request = lax.optimization_barrier((full, request))

    row_index = (
        jnp.arange(high, dtype=jnp.int32)[:, None, None]
        + high * jnp.arange(low, dtype=jnp.int32)[None, None, :]
    )
    col_index = (my_index * cols + jnp.arange(cols, dtype=jnp.int32))[None, :, None]
    row_gain, col_gain = multipliers(row_index, col_index, length)
    row_gain = row_gain * 2.0
    col_gain = col_gain * 2.0
    u_real, u_imag = -row_gain * full[1], row_gain * full[0]
    v_real, v_imag = col_gain * full[1], -col_gain * full[0]

    edge_real = full[0, :, 0].T.reshape(length)
    edge_imag = full[1, :, 0].T.reshape(length)
    flip_real = mirrored(edge_real)
    flip_imag = mirrored(edge_imag)
    ends_real = jnp.stack([(edge_real + flip_real) * 0.5, (edge_imag + flip_imag) * 0.5])
    ends_imag = jnp.stack([(edge_imag - flip_imag) * 0.5, -(edge_real - flip_real) * 0.5])
    end_row, end_col = multipliers(
        jnp.arange(length, dtype=jnp.int32)[None, :],
        jnp.array([0, length // 2], dtype=jnp.int32)[:, None],
        length,
    )
    eu_real, eu_imag = -end_row * ends_imag, end_row * ends_real
    ev_real, ev_imag = end_col * ends_imag, -end_col * ends_real
    on_edge = jnp.logical_and(my_index == 0, jnp.arange(cols) == 0)[None, :, None]

    def place(edge, values):
        return jnp.where(on_edge, edge.reshape(low, high).T[:, None, :], values)

    fields = (
        jnp.stack([place(eu_real[0] - eu_imag[1], u_real), place(eu_imag[0] + eu_real[1], u_imag)]),
        jnp.stack([place(ev_real[0] - ev_imag[1], v_real), place(ev_imag[0] + ev_real[1], v_imag)]),
    )
    untwist = twiddle_table(high, low, length, 1.0)
    real, imag = root(high, high, high, 1.0)
    end_table = np.stack([real, -imag]).astype(np.float32) / (length * length)
    first_k = (jnp.arange(high) == 0)[None, :, None, None]

    def columns_back(field):
        third = dot("cmdb,cknm->dknb", mixing(low, low, low, 1.0), field)
        third = turned(third, untwist, (high, 1, low))
        back = dot("ckda,cknb->adnb", mixing(high, high, high, 1.0), third).astype(BF16)
        if rows % low == 0:
            back = back.reshape(devices, rows // low, 2, cols, low)
        else:
            back = back.reshape(high, 2, cols, low // rows, rows).transpose(0, 3, 1, 2, 4)
            back = back.reshape(devices, 1, 2, cols, rows)
        return lax.all_to_all(back, both, split_axis=0, concat_axis=0)

    def rows_back(back, later, before=None):
        groups, lanes = back.shape[1], back.shape[-1]
        if cols % high == 0:
            back = back.reshape(devices, groups, 2, cols // high, high, lanes)
            table = mixing(half_low, low, low, 1.0).reshape(2, devices, cols // high, 2, low)
            fourth = dot("csmdb,sgcmky->dgkby", table, back.astype(F32))
            nyquist = back[0, :, 1, 0, 0]
        else:
            back = back.reshape(half_low, high // cols, groups, 2, cols, lanes)
            back = back.transpose(0, 2, 3, 1, 4, 5).reshape(half_low, groups, 2, high, lanes)
            fourth = dot("cmdb,mgcky->dgkby", mixing(half_low, low, low, 1.0), back.astype(F32))
            nyquist = back[0, :, 1, 0]
        lift = nyquist.astype(F32)[:, None, None, :] * alternating[None, None, :, None]
        fourth = jnp.stack([fourth[0] + jnp.where(first_k, lift, 0.0), fourth[1]])
        fourth = turned(fourth, untwist, (1, high, low, 1))
        coeffs = dot("cka,cgkby->agby", end_table, fourth).astype(BF16)
        coeffs = coeffs.reshape(group_cols, tile_cols * groups, TILE, lanes)
        if later is not None:
            coeffs, later = lax.optimization_barrier((coeffs, later))
        if before is not None:
            coeffs, before = lax.optimization_barrier((coeffs, before))
        tiles = lax.all_to_all(coeffs, "gy", split_axis=0, concat_axis=0)
        if lanes != TILE:
            parts = TILE // lanes
            tiles = tiles.reshape(group_cols // parts, parts, tile_cols, TILE, lanes)
            tiles = tiles.transpose(0, 2, 3, 1, 4)
        return tiles.reshape(tile_rows * tile_cols, TILE, TILE), later, before

    received = [columns_back(field) for field in fields]
    u_tiles, waiting, _ = rows_back(received[0], received[1])
    v_tiles, _, u_tiles = rows_back(waiting, None, u_tiles)
    tiles = [u_tiles, v_tiles]

    float_total = float_slot.shape[0]
    capacity = 2 * float_total // tile_count
    member = (float_slot[:, None] == jnp.arange(tile_count, dtype=jnp.int32)[None, :]).astype(
        jnp.int32
    )
    slot_rank = jnp.sum((jnp.cumsum(member, axis=0) - member) * member, axis=1)
    placing = float_slot * capacity + slot_rank
    grouped_cell = jnp.zeros((2, tile_count * capacity), jnp.int32).at[:, placing].set(float_cell)
    grouped_cell = grouped_cell.reshape(2, tile_count, capacity).transpose(1, 0, 2)
    grouped_frac = jnp.zeros((2, tile_count * capacity), F32).at[:, placing].set(float_frac)
    grouped_frac = grouped_frac.reshape(2, tile_count, capacity).transpose(1, 0, 2)
    asked = jnp.maximum(request, 0)
    outgoing = jnp.stack([jnp.take(part, asked, axis=0) for part in tiles], axis=1)
    incoming = lax.all_to_all(outgoing, both, split_axis=0, concat_axis=0, tiled=True)
    grouped = slot_velocity(jnp.take(incoming, owner_index, axis=0), grouped_cell, grouped_frac)
    flattened = grouped.transpose(1, 0, 2).reshape(2, tile_count * capacity)
    return jnp.take(flattened, placing, axis=1)


def solution(mesh):
    in_specs = (
        P("gx", "gy"),
        P(("gx", "gy"), None),
        P(("gx", "gy")),
        P(None, ("gx", "gy")),
        P(None, ("gx", "gy")),
    )
    out_specs = P(None, ("gx", "gy"))
    return jax.shard_map(shards, mesh=mesh, in_specs=in_specs, out_specs=out_specs, check_vma=False)
```
